256 devices in a mesh: expert: 8 (over x, core), latent: 32 (over y, z).
Axes of the slice: x: 4, y: 4, z: 8, core: 2. Of those that a mesh axis runs over, the one named last changes fastest.
Arguments:
- tokens: bfloat16 [2048, 2560], P(('expert', 'latent')), may hold values from -6 to 6
- route: int32 [2048, 1], P(('expert', 'latent')), may hold values from 0 to 7; in each aligned block of 8 rows (0 to 7, 8 to 15, ...) at most 2 rows name the same one
- blocks: int32 [2048, 64], P(('expert', 'latent')), may hold values from 0 to 255, all different within a row
- weight: bfloat16 [8, 2560, 32768], P('expert', None, 'latent'), may hold values from -0.125 to 0.125
- enc_bias: float32 [8, 32768], P('expert', 'latent'), may hold values from -3 to 3
- dec_bias: float32 [2560], replicated, may hold values from -3 to 3
Outputs:
- grad_weight: bfloat16 [8, 2560, 32768], P('expert', None, 'latent')
- grad_enc: float32 [8, 32768], P('expert', 'latent')
- grad_dec: float32 [2560], replicated
- loss: float32 [], replicated
The draws below stay inside these ranges and needn't reach their ends.
Inputs may be any that keep to these rules, and one draw needn't show every extreme that they name: `route`: within the rows of one device (aligned blocks of 8 rows) no expert is named by more than 2 rows. Each row lists 64 different blocks.
All inputs are finite; a program needn't handle non-finite values.
Results may differ from the reference program's by a relative error of at most 0.012.
The reference program's roundings to bfloat16 on the way count: a program that leaves them out, or rounds other values in their place, can miss the bound.
Values may be sent and summed in bfloat16 or wider, within the bound.
No kernel may reach another device: no remote copies, remote signals or barrier semaphores. Data moves between devices by JAX's collectives and lax.ppermute only.
A program may use at most 128 MiB of HBM per device.

```python
import math
import jax
import jax.numpy as jnp
import numpy as np
from jax import lax

D = 2560
BLK = 128
K = 64
TOK_DEV = 8
CAP = 2
EXPERTS = 8
LATENTS = 32768
TOKENS = 2048


def levels(own_key, dims, pieces, least, largest):
    def one(axis_at, shards_of):
        heights = jax.random.uniform(jax.random.fold_in(jax.random.fold_in(own_key, 6), axis_at), (shards_of,), jnp.float32, least / len(pieces), largest / len(pieces))
        return jnp.repeat(jnp.exp(heights), dims[axis_at] // shards_of).reshape((-1,) + (1,) * (len(dims) - axis_at - 1))

    level = one(*pieces[0])
    for cut in pieces[1:]:
        level = level * one(*cut)
    return level


def picks_of(key, rows, count, top, lift):
    sequence = jax.random.permutation(jax.random.fold_in(key, 1), count)
    pull = sequence
    for power in range(3):
        pull = pull * pull // count
    pull = pull * lift // count
    tickets = jax.random.randint(jax.random.fold_in(key, 2), (rows, count), 0, 4096) + pull
    sure = jax.random.permutation(jax.random.fold_in(key, 3), rows)[jnp.arange(count) % rows]
    tickets = jnp.where(jnp.arange(rows)[:, None] == sure[None, :], 1 << 14, tickets)
    score = tickets * count + jnp.arange(count)
    return lax.top_k(score.astype(jnp.int32), top)[1].astype(jnp.int32)


def routed_block(rng, own, number, rows, amount, top, limit, lean):
    order = jax.random.permutation(rng, amount)
    heavy_load, common = portions_of(amount, rows * top, limit, lean, True), portions_of(amount, rows * top, limit, lean, False)
    places = jnp.arange(amount)

    def named(tallies, turn):
        used = int((tallies > 0).sum())
        fixed = max(1, used // 4)
        moved = fixed + (places - fixed + turn * (used - fixed)) % max(1, amount - fixed)
        return jnp.zeros((amount,), jnp.int32).at[order[jnp.where(places < fixed, places, moved)]].set(jnp.asarray(tallies, jnp.int32))

    tallies = jnp.where(number % 4 == 0, named(heavy_load, number // 4), named(common, number - number // 4 - 1))
    mixed = jax.random.permutation(jax.random.fold_in(own, 3), amount)
    source_of, taker = mixed[0:amount // 2 * 2:2], mixed[1:amount // 2 * 2:2]
    margin = jnp.minimum(tallies[source_of] - 1, limit - tallies[taker]) // 2
    margin = jnp.where((source_of == order[0]) | (taker == order[0]) | (tallies[taker] == 0), 0, jnp.maximum(margin, 0))
    moved = jax.random.randint(jax.random.fold_in(own, 4), (amount // 2,), 0, 1 << 20) % (margin + 1)
    tallies = tallies.at[source_of].add(-moved).at[taker].add(moved)
    labels = jnp.searchsorted(jnp.cumsum(tallies), jnp.arange(rows * top), side="right").astype(jnp.int32)
    listing = labels.reshape(top, rows).T
    listing = listing[jax.random.permutation(jax.random.fold_in(own, 1), rows)]
    turn = jax.random.randint(jax.random.fold_in(own, 2), (rows, 1), 0, top)
    return jnp.take_along_axis(listing, (jnp.arange(top)[None, :] + turn) % top, axis=1)


def portions_of(count, total, most, skew, full):
    portions = [(1 << 20) // math.isqrt(standing ** skew) + 1 for standing in range(1, count + 1)]
    largest = most if full else min(most, max(-(-total // count), total * portions[0] // sum(portions)))
    least = 1 if total - largest >= count - 1 else 0
    counts, rest = [largest] + [least] * (count - 1), total - largest - least * (count - 1)
    while rest > 0:
        movable = [i for i in range(1, count) if counts[i] < largest] or [i for i in range(1, count) if counts[i] < most]
        pool, budget = sum([portions[i] for i in movable]), rest
        for i in movable:
            extra = min(most - counts[i], max(1, budget * portions[i] // pool), rest)
            counts[i] = counts[i] + extra
            rest = rest - extra
    return np.array(counts)


def scatter_about(rng, extent, spread, limit, cuts=(), kind=jnp.bfloat16):
    level = levels(rng, extent, cuts, -0.22, 0.18) if cuts else 1.0
    values = jax.random.normal(rng, extent, jnp.float32) * spread * level
    return jnp.minimum(jnp.maximum(values, -limit), limit).astype(kind)


def setup_inputs(seed: int = 0) -> dict:
    arg_keys = jax.random.split(jax.random.key(seed), 7)
    tokens = scatter_about(arg_keys[0], (TOKENS, D), 1.0, 6.0, ((0, 256),))
    route_keys = jax.random.split(jax.random.fold_in(arg_keys[1], 1), TOKENS // TOK_DEV)
    route_turns = jax.random.permutation(jax.random.fold_in(arg_keys[1], 3), TOKENS // TOK_DEV)
    route = jax.vmap(lambda own, number: routed_block(jax.random.fold_in(arg_keys[1], 2), own, number, TOK_DEV, EXPERTS, 1, CAP, 2))(route_keys, route_turns).reshape((TOKENS, 1))
    blocks = picks_of(arg_keys[2], TOKENS, LATENTS // BLK, K, 2048)
    weight = scatter_about(arg_keys[3], (EXPERTS, D, LATENTS), D ** -0.5, 0.125, ((0, 8), (2, 32)))
    enc_bias = scatter_about(arg_keys[4], (EXPERTS, LATENTS), 0.5, 3.0, ((0, 8), (1, 32)), jnp.float32)
    dec_bias = scatter_about(arg_keys[5], (D,), 0.5, 3.0, (), jnp.float32)
    return {"tokens": tokens, "route": route, "blocks": blocks, "weight": weight, "enc_bias": enc_bias, "dec_bias": dec_bias}


def expert_table(route):
    sources = TOKENS // TOK_DEV
    expert_of = route[:, 0].astype(jnp.int32).reshape(sources, TOK_DEV)
    one_hot = (expert_of[:, :, None] == jnp.arange(EXPERTS, dtype=jnp.int32)[None, None, :]).astype(jnp.int32)
    earlier = jnp.sum((jnp.cumsum(one_hot, axis=1) - one_hot) * one_hot, axis=2).astype(jnp.int32)
    position = (jnp.arange(sources, dtype=jnp.int32)[:, None] * CAP + earlier).astype(jnp.int32)
    token_ids = jnp.arange(TOKENS, dtype=jnp.int32).reshape(sources, TOK_DEV)
    table = jnp.full((EXPERTS, sources * CAP), -1, jnp.int32)
    return table.at[expert_of.reshape(-1), position.reshape(-1)].set(token_ids.reshape(-1))


def reference(tokens, route, blocks, weight, enc_bias, dec_bias):
    table = expert_table(route)
    block_count = LATENTS // BLK

    def one_expert(operands):
        token_ids, weights_here, bias_here = operands
        valid = (token_ids >= 0).astype(jnp.float32)
        safe_ids = jnp.maximum(token_ids, 0).astype(jnp.int32)
        rows_f32 = tokens[safe_ids].astype(jnp.float32) * valid[:, None]
        listed = blocks[safe_ids]
        chosen = jnp.any(listed[:, :, None] == jnp.arange(block_count, dtype=jnp.int32)[None, None, :], axis=1)
        mask = jnp.repeat(chosen.astype(jnp.float32) * valid[:, None], BLK, axis=1)
        shifted = (rows_f32 - dec_bias).astype(jnp.bfloat16)
        pre_act = jnp.dot(shifted, weights_here, preferred_element_type=jnp.float32) + bias_here
        active = jnp.maximum(pre_act, 0.0) * mask
        active_bf = active.astype(jnp.bfloat16)
        recon = jnp.dot(active_bf, weights_here.T, preferred_element_type=jnp.float32) + dec_bias
        error = (recon - rows_f32) * valid[:, None]
        error_bf = error.astype(jnp.bfloat16)
        grad_act = jnp.dot(error_bf, weights_here, preferred_element_type=jnp.float32)
        grad_pre = grad_act * (pre_act > 0.0).astype(jnp.float32) * mask
        grad_pre_bf = grad_pre.astype(jnp.bfloat16)
        grad_here = jnp.dot(shifted.T, grad_pre_bf, preferred_element_type=jnp.float32)
        grad_here = grad_here + jnp.dot(error_bf.T, active_bf, preferred_element_type=jnp.float32)
        grad_bias = jnp.sum(grad_pre, axis=0)
        pulled = jnp.dot(weights_here, grad_bias.astype(jnp.bfloat16), preferred_element_type=jnp.float32)
        return grad_here.astype(jnp.bfloat16), grad_bias, jnp.sum(error, axis=0) - pulled, 0.5 * jnp.sum(error * error)

    grad_weight, grad_enc, dec_terms, loss_terms = lax.map(one_expert, (table, weight, enc_bias))
    grad_dec = jnp.sum(dec_terms, axis=0)
    loss = jnp.sum(loss_terms) / TOKENS
    return (grad_weight, grad_enc, grad_dec, loss)
```

```python
import jax
import jax.numpy as jnp
from jax import lax
from jax.experimental import pallas as pl
from jax.experimental.pallas import tpu as pltpu
from jax.sharding import PartitionSpec as P

BLK = 128
CAP = 2
NY, NZ = 4, 8
ZS = (1, 7, 2, 6, 3, 5, 4)
STEP = 256
WIDE = 512
F32, BF16 = jnp.float32, jnp.bfloat16
PAIR = (((1,), (1,)), ((), ()))
ROWS = (((0,), (0,)), ((), ()))
ONCHIP = pl.BlockSpec(memory_space=pltpu.VMEM)


def along(dy, dz):
    return [
        (y * NZ + z, (y + dy) % NY * NZ + (z + dz) % NZ) for y in range(NY) for z in range(NZ)
    ]


def send(v, dy, dz):
    return lax.ppermute(v, "latent", along(dy, dz))


def right(v):
    return send(v, 1, 0)


def left(v):
    return send(v, -1, 0)


def struct(rows, cols, dtype):
    return jax.ShapeDtypeStruct((rows, cols), dtype)


def call(body, outs, args, name):
    return pl.pallas_call(
        body,
        out_shape=outs,
        name=name,
        in_specs=[ONCHIP] * len(args),
        out_specs=jax.tree.map(lambda _: ONCHIP, outs),
        compiler_params=pltpu.CompilerParams(vmem_limit_bytes=4 << 20),
    )(*args)


def place_rows(tokens, route, blocks):
    count, width = tokens.shape
    n = lax.axis_size("expert")

    def body(tok, row, ids, out):
        i = lax.broadcasted_iota(jnp.int32, (count, count), 0)
        j = lax.broadcasted_iota(jnp.int32, (count, count), 1)
        expert = row[...].astype(F32)
        across = jnp.broadcast_to(expert, (count, count))
        down = jnp.sum(jnp.where(i == j, across, 0.0), axis=1, keepdims=True)
        same = jnp.where((down == across) & (i < j), 1.0, 0.0)
        target = expert * CAP + jnp.sum(same, axis=0, keepdims=True)
        slot = lax.broadcasted_iota(jnp.int32, (n * CAP, count), 0).astype(F32)
        place = jnp.where(slot == target, 1.0, 0.0).astype(BF16)
        rows = jnp.dot(place, tok[...], preferred_element_type=F32).astype(BF16)
        named = (ids[...] + 1).astype(F32).astype(BF16)
        listed = jnp.dot(place, named, preferred_element_type=F32).astype(BF16)
        for e in range(n):
            at = slice(e * CAP, (e + 1) * CAP)
            out[e, :, :width] = rows[at]
            out[e, :, width:] = jnp.zeros((CAP, BLK), BF16)
            out[e, :, width : width + ids.shape[1]] = listed[at]

    return call(
        body,
        jax.ShapeDtypeStruct((n, CAP, width + BLK), BF16),
        (tokens, route.reshape(1, count), blocks),
        "place_rows",
    )


def shift_rows(rows, dec):
    width = dec.shape[1]
    n = rows.shape[0]

    def body(x, d, out, kept):
        for e in range(n):
            at = slice(e * CAP, (e + 1) * CAP)
            kept[at, :] = x[e]
        out[:, :width] = (kept[:, :width].astype(F32) - d[...]).astype(BF16)
        out[:, width:] = kept[:, width:]

    shape = struct(n * CAP, rows.shape[2], BF16)
    return call(body, (shape, shape), (rows, dec), "shift_rows")


def join(parts):
    half = len(parts) // 2
    n, cols = parts[0].shape

    def body(*refs):
        for k in range(2 * half):
            refs[2 * half + k // half][k % half * n : (k % half + 1) * n, :] = refs[k][...]

    return call(body, (struct(n * half, cols, BF16),) * 2, parts, "join")


def gather_z(v):
    return join([v] + [send(v, 0, dz) for dz in ZS])


def ring(a, b):
    r0, l1, r1, l0 = right(a), left(b), right(b), left(a)
    return (r0, r1, l0, l1), (right(r0), left(l1))


def big(body, outs, args, name, flops, in_specs=None):
    return pl.pallas_call(
        body,
        out_shape=outs,
        name=name,
        in_specs=in_specs or [ONCHIP] * len(args),
        out_specs=[ONCHIP] * len(outs),
        compiler_params=pltpu.CompilerParams(vmem_limit_bytes=12 << 20),
        cost_estimate=pl.CostEstimate(flops=flops, bytes_accessed=flops // 256, transcendentals=0),
    )(*args)


def forward(parts, weight, bias, index, out_types, name):
    n = len(parts)
    piece = parts[0].shape[0]
    rows = n * piece
    width, latents = weight.shape
    per = STEP // BLK

    def body(*refs):
        idx, ins, w, b = refs[0], refs[1 : 1 + n], refs[1 + n], refs[2 + n]
        s, a, m = refs[3 + n : 6 + n]
        outs = refs[6 + n :]
        for k in range(n):
            s[k * piece : (k + 1) * piece, :] = ins[k][:, :width]
        named = jnp.concatenate([r[:, width:] for r in ins], axis=0).astype(F32)
        for c in range(latents // STEP):
            at = slice(c * STEP, (c + 1) * STEP)
            pre = jnp.dot(s[...], w[:, at], preferred_element_type=F32) + b[:, at]
            base = (idx[0] * (latents // BLK) + c * per + 1).astype(F32)
            hits = []
            for j in range(per):
                found = jnp.max(jnp.where(named == base + j, 1.0, 0.0), axis=1, keepdims=True)
                hits.append(jnp.broadcast_to(found, (rows, BLK)))
            gate = jnp.where(pre > 0.0, jnp.concatenate(hits, axis=1), 0.0)
            a[:, at] = (jnp.maximum(pre, 0.0) * gate).astype(BF16)
            m[:, at] = gate.astype(BF16)
        for d in range(width // WIDE):
            at = slice(d * WIDE, (d + 1) * WIDE)
            part = lax.dot_general(a[...], w[at, :], PAIR, preferred_element_type=F32)
            for k in range(n):
                outs[k][:, at] = part[k * piece : (k + 1) * piece].astype(outs[k].dtype)

    specs = [pl.BlockSpec(memory_space=pltpu.SMEM)]
    specs += [ONCHIP] * (n + 2)
    outs = [
        struct(rows, width, BF16),
        struct(rows, latents, BF16),
        struct(rows, latents, BF16),
    ] + [struct(piece, width, t) for t in out_types]
    flops = 4 * rows * width * latents
    return big(body, outs, (index, *parts, weight, bias), name, flops, specs)


def backward(parts, weight, gate, bias, terms, name):
    n = len(parts)
    piece = parts[0].shape[0]
    rows = n * piece
    width, latents = weight.shape
    last = terms is not None

    def body(*refs):
        ins, w, m, prior = refs[:n], refs[n], refs[n + 1], refs[n + 2]
        rest = refs[n + 3 :]
        if last:
            t, e, g, total, vec = rest
        else:
            e, g, total = rest
        for k in range(n):
            e[k * piece : (k + 1) * piece, :] = ins[k][...]
        for c in range(latents // STEP):
            at = slice(c * STEP, (c + 1) * STEP)
            grad = jnp.dot(e[...], w[:, at], preferred_element_type=F32) * m[:, at].astype(F32)
            g[:, at] = grad.astype(BF16)
            total[:, at] = jnp.sum(grad, axis=0, keepdims=True) + prior[:, at]
        if last:
            column = total[...].astype(BF16).astype(F32)
            column = jnp.broadcast_to(column, (8, latents)).astype(BF16)
            for d in range(width // WIDE):
                at = slice(d * WIDE, (d + 1) * WIDE)
                pulled = lax.dot_general(column, w[at, :], PAIR, preferred_element_type=F32)
                vec[:, at] = t[:, at] - pulled[:1]
            vec[:, width:] = t[:, width:]

    outs = [struct(rows, width, BF16), struct(rows, latents, BF16), struct(1, latents, F32)]
    args = (*parts, weight, gate, bias)
    if last:
        outs += [struct(*terms.shape, F32)]
        args += (terms,)
    return big(body, outs, args, name, 2 * rows * width * latents)


def split_sum(own, a1, b1, a2, b2, share):
    half, width = a1.shape
    n = 2 * half // share

    def body(pa, pb, w, x, y, z, *outs):
        for k in range(n):
            lo = k * share % half
            p, u, v = (pa, w, x) if k * share < half else (pb, y, z)
            rows = pl.ds(lo, share)
            total = p[rows, :] + u[rows, :].astype(F32) + v[rows, :].astype(F32)
            outs[k][...] = total.astype(outs[k].dtype)

    outs = (struct(share, width, F32),) + (struct(share, width, BF16),) * (n - 1)
    return call(body, outs, (*own, a1, b1, a2, b2), "split_sum")


def form_error(own, others, rows, dec):
    share, width = own.shape

    def body(o, *refs):
        x, d, err, terms = refs[-4:]
        recon = o[...]
        for r in refs[:-4]:
            recon = recon + r[...].astype(F32)
        held = jnp.where(x[:, width : width + 1].astype(F32) > 0.0, 1.0, 0.0)
        e = (recon + d[...] - x[:, :width].astype(F32)) * held
        err[...] = e.astype(BF16)
        terms[:, :width] = jnp.sum(e, axis=0, keepdims=True)
        loss = 0.5 * jnp.sum(jnp.sum(e * e, axis=1, keepdims=True), axis=0, keepdims=True)
        terms[:, width:] = jnp.broadcast_to(loss, (1, BLK))

    return call(
        body,
        (struct(share, width, BF16), struct(1, width + BLK, F32)),
        (own, *others, rows, dec),
        "form_error",
    )


def weight_grad(buffer, step, tile, groups, width, latents):
    s0, e0, g0, a0, s1, g1, e1, a1, s2, e2, g2, a2 = groups
    names = [s0, e0, s1, e1, s2, e2, g0, a0, g1, a1, g2, a2]

    def body(*refs):
        s0, e0, s1, e1, s2, e2, g0, a0, g1, a1, g2, a2 = refs[:12]
        out = refs[-1]
        at = pl.ds(step * tile + pl.program_id(0) * STEP, STEP)
        dot = lambda u, v: lax.dot_general(u, v, ROWS, preferred_element_type=F32)
        tall = lambda u, v: jnp.concatenate([u[:, at], v[:, at]], axis=0)
        flat = lambda u, v: jnp.concatenate([u[...], v[...]], axis=0)
        total = dot(tall(s0, e0), flat(g0, a0))
        total += dot(s1[:, at], g1[...])
        total += dot(e1[:, at], a1[...])
        total += dot(tall(s2, e2), flat(g2, a2))
        out[...] = total.astype(BF16)

    rows = sum(v.shape[0] for v in names[:6])
    kept = [] if buffer is None else [buffer]
    per = tile // STEP
    return pl.pallas_call(
        body,
        name="weight_grad",
        grid=(per,),
        in_specs=[ONCHIP] * 12 + [pl.BlockSpec(memory_space=pl.ANY)] * len(kept),
        out_specs=pl.BlockSpec((STEP, latents), lambda c: (per * step + c, 0)),
        out_shape=struct(width, latents, BF16),
        input_output_aliases={12: 0} if kept else {},
        compiler_params=pltpu.CompilerParams(vmem_limit_bytes=8 << 20),
        cost_estimate=pl.CostEstimate(
            flops=2 * rows * tile * latents, bytes_accessed=4 * rows * latents, transcendentals=0
        ),
    )(*names, *kept)


def shards(tokens, route, blocks, weight, enc_bias, dec_bias):
    n_expert = lax.axis_size("expert")
    n_latent = lax.axis_size("latent")
    count, width = tokens.shape
    w = weight[0]
    latents = w.shape[1]
    share = n_expert * CAP
    dec = dec_bias[None]
    index = lax.axis_index("latent").astype(jnp.int32)[None]

    rows = place_rows(tokens, route, blocks)
    rows = lax.all_to_all(rows, "expert", split_axis=0, concat_axis=0, tiled=True)
    parcel, rows = shift_rows(rows, dec)
    za, zb = gather_z(parcel)
    near, far = ring(za, zb)
    s0, a0, m0, p0a, p0b = forward((za, zb), w, enc_bias, index, (F32, F32), "forward_own")
    index, _ = lax.optimization_barrier((index, p0a))
    s1, a1, m1, m_h1, m_h2, p_h1, p_h2 = forward(
        near, w, enc_bias, index, (BF16, F32, F32, BF16), "forward_near"
    )
    index, _ = lax.optimization_barrier((index, p_h1))
    s2, a2, m2, o_h1, o_h2 = forward(far, w, enc_bias, index, (BF16, BF16), "forward_far")
    in_a2, in_b1 = right(p_h2), left(m_h1)
    x1, x2 = right(o_h1), left(o_h2)
    in_a1 = right((p_h1 + x1.astype(F32)).astype(BF16))
    in_b2 = left((m_h2 + x2.astype(F32)).astype(BF16))
    pieces = split_sum((p0a, p0b), in_a1, in_b1, in_a2, in_b2, share)
    others = [send(v, 0, -dz) for v, dz in zip(pieces[1:], ZS)]
    error, terms = form_error(pieces[0], others, rows, dec)

    ea, eb = gather_z(error)
    e_near, e_far = ring(ea, eb)
    zero = jnp.zeros((1, latents), F32)
    e0, g0, bias = backward((ea, eb), w, m0, zero, None, "backward_own")
    e1, g1, bias = backward(e_near, w, m1, bias, None, "backward_near")
    e2, g2, bias, vec = backward(e_far, w, m2, bias, terms, "backward_far")

    groups = (s0, e0, g0, a0, s1, g1, e1, a1, s2, e2, g2, a2)
    tile = 512
    parts = width // tile
    grad = None
    both = ("expert", "latent")
    for k, (one, two) in enumerate(((32, 64), (128, 4), (1, 2), (8, 16))):
        moved = [
            lax.ppermute(vec, both, [(i, i ^ m) for i in range(n_expert * n_latent)])
            for m in (one, two, one | two)
        ]
        for p in range(parts * k // 4, parts * (k + 1) // 4):
            grad = weight_grad(grad, p, tile, groups, width, latents)
        vec = (vec + moved[0]) + (moved[1] + moved[2])
        vec, grad = lax.optimization_barrier((vec, grad))
    loss = vec[0, width] / (count * n_expert * n_latent)
    return (grad[None], bias, vec[0, :width], loss)


def solution(mesh):
    return jax.shard_map(
        shards,
        mesh=mesh,
        in_specs=(
            P(("expert", "latent"), None),
            P(("expert", "latent"), None),
            P(("expert", "latent"), None),
            P("expert", None, "latent"),
            P("expert", "latent"),
            P(),
        ),
        out_specs=(P("expert", None, "latent"), P("expert", "latent"), P(), P()),
        check_vma=False,
    )
```

```python
import jax
import jax.numpy as jnp
from jax import lax
from jax.experimental import pallas as pl
from jax.experimental.pallas import tpu as pltpu
from jax.sharding import PartitionSpec as P

BLK = 128
CAP = 2
NY, NZ = 4, 8
STEP = 256
WIDE = 512
F32, BF16 = jnp.float32, jnp.bfloat16
PAIR = (((1,), (1,)), ((), ()))
ROWS = (((0,), (0,)), ((), ()))
ONCHIP = pl.BlockSpec(memory_space=pltpu.VMEM)


def along(dy, dz):
    return [
        (y * NZ + z, (y + dy) % NY * NZ + (z + dz) % NZ) for y in range(NY) for z in range(NZ)
    ]


def send(v, dy, dz):
    return lax.ppermute(v, "latent", along(dy, dz))


def right(v):
    return send(v, 1, 0)


def left(v):
    return send(v, -1, 0)


def struct(rows, cols, dtype):
    return jax.ShapeDtypeStruct((rows, cols), dtype)


def call(body, outs, args, name, onchip=True):
    if not onchip:
        return pl.pallas_call(body, out_shape=outs, name=name)(*args)
    return pl.pallas_call(
        body,
        out_shape=outs,
        name=name,
        in_specs=[ONCHIP] * len(args),
        out_specs=jax.tree.map(lambda _: ONCHIP, outs),
        compiler_params=pltpu.CompilerParams(vmem_limit_bytes=4 << 20),
    )(*args)


def place_rows(tokens, route, blocks):
    count, width = tokens.shape
    n = lax.axis_size("expert")

    def body(tok, row, ids, out):
        i = lax.broadcasted_iota(jnp.int32, (count, count), 0)
        j = lax.broadcasted_iota(jnp.int32, (count, count), 1)
        expert = row[...].astype(F32)
        across = jnp.broadcast_to(expert, (count, count))
        down = jnp.sum(jnp.where(i == j, across, 0.0), axis=1, keepdims=True)
        same = jnp.where((down == across) & (i < j), 1.0, 0.0)
        target = expert * CAP + jnp.sum(same, axis=0, keepdims=True)
        slot = lax.broadcasted_iota(jnp.int32, (n * CAP, count), 0).astype(F32)
        place = jnp.where(slot == target, 1.0, 0.0).astype(BF16)
        rows = jnp.dot(place, tok[...], preferred_element_type=F32).astype(BF16)
        named = (ids[...] + 1).astype(F32).astype(BF16)
        listed = jnp.dot(place, named, preferred_element_type=F32).astype(BF16)
        for e in range(n):
            at = slice(e * CAP, (e + 1) * CAP)
            out[e, :, :width] = rows[at]
            out[e, :, width:] = jnp.zeros((CAP, BLK), BF16)
            out[e, :, width : width + ids.shape[1]] = listed[at]

    return call(
        body,
        jax.ShapeDtypeStruct((n, CAP, width + BLK), BF16),
        (tokens, route.reshape(1, count), blocks),
        "place_rows",
        False,
    )


def shift_rows(rows, dec):
    width = dec.shape[1]
    n = rows.shape[0]

    def body(x, d, out, kept):
        for e in range(n):
            at = slice(e * CAP, (e + 1) * CAP)
            kept[at, :] = x[e]
        out[:, :width] = (kept[:, :width].astype(F32) - d[...]).astype(BF16)
        out[:, width:] = kept[:, width:]

    shape = struct(n * CAP, rows.shape[2], BF16)
    return call(body, (shape, shape), (rows, dec), "shift_rows")


def join(outs, args, name):
    n = len(args)

    def body(*refs):
        for out, picks in zip(refs[n:], outs):
            at = 0
            for k in picks:
                rows = args[k].shape[0]
                out[at : at + rows, :] = refs[k][...]
                at += rows

    cols = args[0].shape[1]
    shapes = [struct(sum(args[k].shape[0] for k in picks), cols, BF16) for picks in outs]
    return call(body, shapes, args, name)


def gather_z(v):
    across, below, above = send(v, 0, 4), send(v, 0, 2), send(v, 0, -2)
    (duo,) = join(((0, 1),), (v, across), "join_duo")
    low, high = send(duo, 0, 1), send(duo, 0, -1)
    return join(((0, 1, 2, 3), (4, 5)), (v, across, below, above, low, high), "join")


def ring(a, b):
    r0, l1, r1, l0 = right(a), left(b), right(b), left(a)
    return (r0, r1, l0, l1), (right(r0), left(l1))


def big(body, outs, args, name, flops, in_specs=None):
    return pl.pallas_call(
        body,
        out_shape=outs,
        name=name,
        in_specs=in_specs or [ONCHIP] * len(args),
        out_specs=[ONCHIP] * len(outs),
        compiler_params=pltpu.CompilerParams(vmem_limit_bytes=12 << 20),
        cost_estimate=pl.CostEstimate(flops=flops, bytes_accessed=flops // 256, transcendentals=0),
    )(*args)


def forward(parts, weight, bias, index, out_types, name):
    n = len(parts)
    piece = parts[0].shape[0]
    rows = n * piece
    width, latents = weight.shape
    per = STEP // BLK

    def body(*refs):
        idx, ins, w, b = refs[0], refs[1 : 1 + n], refs[1 + n], refs[2 + n]
        s, a, m = refs[3 + n : 6 + n]
        outs = refs[6 + n :]
        for k in range(n):
            s[k * piece : (k + 1) * piece, :] = ins[k][:, :width]
        named = jnp.concatenate([r[:, width:] for r in ins], axis=0).astype(F32)
        for c in range(latents // STEP):
            at = slice(c * STEP, (c + 1) * STEP)
            pre = jnp.dot(s[...], w[:, at], preferred_element_type=F32) + b[:, at]
            base = (idx[0] * (latents // BLK) + c * per + 1).astype(F32)
            hits = []
            for j in range(per):
                found = jnp.max(jnp.where(named == base + j, 1.0, 0.0), axis=1, keepdims=True)
                hits.append(jnp.broadcast_to(found, (rows, BLK)))
            gate = jnp.where(pre > 0.0, jnp.concatenate(hits, axis=1), 0.0)
            a[:, at] = (jnp.maximum(pre, 0.0) * gate).astype(BF16)
            m[:, at] = gate.astype(BF16)
        for d in range(width // WIDE):
            at = slice(d * WIDE, (d + 1) * WIDE)
            part = lax.dot_general(a[...], w[at, :], PAIR, preferred_element_type=F32)
            for k in range(n):
                outs[k][:, at] = part[k * piece : (k + 1) * piece].astype(outs[k].dtype)

    specs = [pl.BlockSpec(memory_space=pltpu.SMEM)]
    specs += [ONCHIP] * (n + 2)
    outs = [
        struct(rows, width, BF16),
        struct(rows, latents, BF16),
        struct(rows, latents, BF16),
    ] + [struct(piece, width, t) for t in out_types]
    flops = 4 * rows * width * latents
    return big(body, outs, (index, *parts, weight, bias), name, flops, specs)


def backward(parts, weight, gate, bias, terms, name, after=()):
    n = len(parts)
    piece = parts[0].shape[0]
    rows = n * piece
    width, latents = weight.shape
    last = terms is not None

    def body(*refs):
        ins, w, m, prior = refs[:n], refs[n], refs[n + 1], refs[n + 2]
        rest = refs[n + 3 + len(after) :]
        if last:
            t, e, g, total, vec = rest
        else:
            e, g, total = rest
        for k in range(n):
            e[k * piece : (k + 1) * piece, :] = ins[k][...]
        for c in range(latents // STEP):
            at = slice(c * STEP, (c + 1) * STEP)
            grad = jnp.dot(e[...], w[:, at], preferred_element_type=F32) * m[:, at].astype(F32)
            g[:, at] = grad.astype(BF16)
            total[:, at] = jnp.sum(grad, axis=0, keepdims=True) + prior[:, at]
        if last:
            column = total[...].astype(BF16).astype(F32)
            column = jnp.broadcast_to(column, (8, latents)).astype(BF16)
            for d in range(width // WIDE):
                at = slice(d * WIDE, (d + 1) * WIDE)
                pulled = lax.dot_general(column, w[at, :], PAIR, preferred_element_type=F32)
                vec[:, at] = t[:, at] - pulled[:1]
            vec[:, width:] = t[:, width:]

    outs = [struct(rows, width, BF16), struct(rows, latents, BF16), struct(1, latents, F32)]
    args = (*parts, weight, gate, bias, *after)
    if last:
        outs += [struct(*terms.shape, F32)]
        args += (terms,)
    return big(body, outs, args, name, 2 * rows * width * latents)


def split_sum(own, a1, b1, a2, b2):
    half, width = a1.shape
    n = half // 4

    def body(pa, pb, w, x, y, z, mine, across, below, above, low, high):
        def rows(p, u, v, lo, count):
            at = slice(lo * n, (lo + count) * n)
            return p[at, :] + u[at, :].astype(F32) + v[at, :].astype(F32)

        low[...] = rows(pb, y, z, 0, 2).astype(BF16)
        high[...] = rows(pb, y, z, 2, 2).astype(BF16)
        below[...] = rows(pa, w, x, 2, 1).astype(BF16)
        above[...] = rows(pa, w, x, 3, 1).astype(BF16)
        mine[...] = rows(pa, w, x, 0, 1)
        across[...] = rows(pa, w, x, 1, 1)

    outs = [struct(n, width, F32)] * 2 + [struct(n, width, BF16)] * 2
    outs += [struct(2 * n, width, BF16)] * 2
    return call(body, outs, (*own, a1, b1, a2, b2), "split_sum")


def fold(across, low, high):
    n, width = across.shape

    def body(p, u, v, out):
        out[...] = (p[...] + u[n:, :].astype(F32) + v[n:, :].astype(F32)).astype(BF16)

    return call(body, struct(n, width, BF16), (across, low, high), "fold")


def form_error(own, others, rows, dec):
    share, width = own.shape

    def body(o, *refs):
        x, d, err, terms = refs[-4:]
        recon = o[...]
        for r in refs[:-4]:
            recon = recon + r[:share, :].astype(F32)
        held = jnp.where(x[:, width : width + 1].astype(F32) > 0.0, 1.0, 0.0)
        e = (recon + d[...] - x[:, :width].astype(F32)) * held
        err[...] = e.astype(BF16)
        terms[:, :width] = jnp.sum(e, axis=0, keepdims=True)
        loss = 0.5 * jnp.sum(jnp.sum(e * e, axis=1, keepdims=True), axis=0, keepdims=True)
        terms[:, width:] = jnp.broadcast_to(loss, (1, BLK))

    return call(
        body,
        (struct(share, width, BF16), struct(1, width + BLK, F32)),
        (own, *others, rows, dec),
        "form_error",
    )


def add_grad(acc, pairs, name):
    width, latents = pairs[0][0].shape[1], pairs[0][1].shape[1]
    flat = [v for pair in pairs for v in pair]
    kept = [] if acc is None else [acc]

    def body(*refs):
        out, mark = refs[-2:]
        mark[...] = jnp.zeros_like(mark)
        for d in range(width // STEP):
            at = slice(d * STEP, (d + 1) * STEP)
            total = refs[len(flat)][at, :] if kept else None
            for k in range(0, len(flat), 2):
                part = lax.dot_general(
                    refs[k][:, at], refs[k + 1][...], ROWS, preferred_element_type=F32
                )
                total = part if total is None else total + part
            out[at, :] = total

    rows = sum(u.shape[0] for u, _ in pairs)
    return pl.pallas_call(
        body,
        out_shape=[struct(width, latents, F32), struct(8, BLK, F32)],
        name=name,
        in_specs=[ONCHIP] * (len(flat) + len(kept)),
        out_specs=[ONCHIP] * 2,
        input_output_aliases={len(flat): 0} if kept else {},
        compiler_params=pltpu.CompilerParams(vmem_limit_bytes=12 << 20),
        cost_estimate=pl.CostEstimate(
            flops=2 * rows * width * latents, bytes_accessed=8 * width * latents, transcendentals=0
        ),
    )(*flat, *kept)


def finish_grad(buffer, first, count, acc, pairs):
    width, latents = acc.shape
    flat = [v for pair in pairs for v in pair]
    n = len(flat)
    kept = [] if buffer is None else [buffer]

    def body(*refs):
        at = pl.ds((first + pl.program_id(0)) * STEP, STEP)
        left_side = jnp.concatenate([refs[k][:, at] for k in range(0, n, 2)], axis=0)
        right_side = jnp.concatenate([refs[k][...] for k in range(1, n, 2)], axis=0)
        part = lax.dot_general(left_side, right_side, ROWS, preferred_element_type=F32)
        refs[-1][...] = (refs[n][at, :] + part).astype(BF16)

    rows = sum(u.shape[0] for u, _ in pairs)
    return pl.pallas_call(
        body,
        name="finish_grad",
        grid=(count,),
        in_specs=[ONCHIP] * (n + 1) + [pl.BlockSpec(memory_space=pl.ANY)] * len(kept),
        out_specs=pl.BlockSpec((STEP, latents), lambda c: (first + c, 0)),
        out_shape=struct(width, latents, BF16),
        input_output_aliases={n + 1: 0} if kept else {},
        compiler_params=pltpu.CompilerParams(vmem_limit_bytes=8 << 20),
        cost_estimate=pl.CostEstimate(
            flops=2 * rows * count * STEP * latents,
            bytes_accessed=6 * count * STEP * latents,
            transcendentals=0,
        ),
    )(*flat, acc, *kept)


def shards(tokens, route, blocks, weight, enc_bias, dec_bias):
    n_expert = lax.axis_size("expert")
    n_latent = lax.axis_size("latent")
    count, width = tokens.shape
    w = weight[0]
    latents = w.shape[1]
    share = n_expert * CAP
    dec = dec_bias[None]
    index = lax.axis_index("latent").astype(jnp.int32)[None]

    rows = place_rows(tokens, route, blocks)
    rows = lax.all_to_all(rows, "expert", split_axis=0, concat_axis=0, tiled=True)
    parcel, rows = shift_rows(rows, dec)
    za, zb = gather_z(parcel)
    near, far = ring(za, zb)
    s0, a0, m0, p0a, p0b = forward((za, zb), w, enc_bias, index, (F32, F32), "forward_own")
    index, _ = lax.optimization_barrier((index, p0a))
    s1, a1, m1, m_h1, m_h2, p_h1, p_h2 = forward(
        near, w, enc_bias, index, (BF16, F32, F32, BF16), "forward_near"
    )
    index, _ = lax.optimization_barrier((index, p_h1))
    s2, a2, m2, o_h1, o_h2 = forward(far, w, enc_bias, index, (BF16, BF16), "forward_far")
    in_a2, in_b1 = right(p_h2), left(m_h1)
    x1, x2 = right(o_h1), left(o_h2)
    in_a1 = right((p_h1 + x1.astype(F32)).astype(BF16))
    in_b2 = left((m_h2 + x2.astype(F32)).astype(BF16))
    mine, across, below, above, low, high = split_sum((p0a, p0b), in_a1, in_b1, in_a2, in_b2)
    low, high = send(low, 0, -1), send(high, 0, 1)
    others = (low, high, send(below, 0, -2), send(above, 0, 2))
    others += (send(fold(across, low, high), 0, 4),)
    error, terms = form_error(mine, others, rows, dec)

    ea, eb = gather_z(error)
    e_near, e_far = ring(ea, eb)
    zero = jnp.zeros((1, latents), F32)
    e0, g0, bias = backward((ea, eb), w, m0, zero, None, "backward_own")
    acc, mark = add_grad(None, ((s0, g0), (e0, a0)), "add_grad_own")
    e1, g1, bias = backward(e_near, w, m1, bias, None, "backward_near", (mark,))
    acc, mark = add_grad(acc, ((s1, g1), (e1, a1)), "add_grad_near")
    e2, g2, bias, vec = backward(e_far, w, m2, bias, terms, "backward_far", (mark,))

    tiles = width // STEP
    grad = None
    both = ("expert", "latent")
    stages = ((64, 128), (8, 16), (1, 2), (32,), (4,))
    for k, bits in enumerate(stages):
        masks = bits + ((bits[0] | bits[1],) if len(bits) == 2 else ())
        moved = [
            lax.ppermute(vec, both, [(i, i ^ m) for i in range(n_expert * n_latent)])
            for m in masks
        ]
        start, stop = tiles * k // len(stages), tiles * (k + 1) // len(stages)
        grad = finish_grad(grad, start, stop - start, acc, ((s2, g2), (e2, a2)))
        vec = vec + moved[0]
        if len(bits) == 2:
            vec = vec + (moved[1] + moved[2])
        vec, grad = lax.optimization_barrier((vec, grad))
    loss = vec[0, width] / (count * n_expert * n_latent)
    return (grad[None], bias, vec[0, :width], loss)


def solution(mesh):
    return jax.shard_map(
        shards,
        mesh=mesh,
        in_specs=(
            P(("expert", "latent"), None),
            P(("expert", "latent"), None),
            P(("expert", "latent"), None),
            P("expert", None, "latent"),
            P("expert", "latent"),
            P(),
        ),
        out_specs=(P("expert", None, "latent"), P("expert", "latent"), P(), P()),
        check_vma=False,
    )
```

```python
import jax
import jax.numpy as jnp
from jax import lax
from jax.experimental import pallas as pl
from jax.experimental.pallas import tpu as pltpu
from jax.sharding import PartitionSpec as P

BLK = 128
CAP = 2
NY, NZ = 4, 8
STEP = 256
WIDE = 512
F32, BF16 = jnp.float32, jnp.bfloat16
PAIR = (((1,), (1,)), ((), ()))
ROWS = (((0,), (0,)), ((), ()))
ONCHIP = pl.BlockSpec(memory_space=pltpu.VMEM)


def along(dy, dz):
    return [
        (y * NZ + z, (y + dy) % NY * NZ + (z + dz) % NZ) for y in range(NY) for z in range(NZ)
    ]


def send(v, dy, dz):
    return lax.ppermute(v, "latent", along(dy, dz))


def right(v):
    return send(v, 1, 0)


def left(v):
    return send(v, -1, 0)


def struct(rows, cols, dtype):
    return jax.ShapeDtypeStruct((rows, cols), dtype)


def call(body, outs, args, name, onchip=True):
    if not onchip:
        return pl.pallas_call(body, out_shape=outs, name=name)(*args)
    return pl.pallas_call(
        body,
        out_shape=outs,
        name=name,
        in_specs=[ONCHIP] * len(args),
        out_specs=jax.tree.map(lambda _: ONCHIP, outs),
        compiler_params=pltpu.CompilerParams(vmem_limit_bytes=4 << 20),
    )(*args)


def place_rows(tokens, route, blocks):
    count, width = tokens.shape
    n = lax.axis_size("expert")

    def body(tok, row, ids, out):
        i = lax.broadcasted_iota(jnp.int32, (count, count), 0)
        j = lax.broadcasted_iota(jnp.int32, (count, count), 1)
        expert = row[...].astype(F32)
        across = jnp.broadcast_to(expert, (count, count))
        down = jnp.sum(jnp.where(i == j, across, 0.0), axis=1, keepdims=True)
        same = jnp.where((down == across) & (i < j), 1.0, 0.0)
        target = expert * CAP + jnp.sum(same, axis=0, keepdims=True)
        slot = lax.broadcasted_iota(jnp.int32, (n * CAP, count), 0).astype(F32)
        place = jnp.where(slot == target, 1.0, 0.0).astype(BF16)
        rows = jnp.dot(place, tok[...], preferred_element_type=F32).astype(BF16)
        named = (ids[...] + 1).astype(F32).astype(BF16)
        listed = jnp.dot(place, named, preferred_element_type=F32).astype(BF16)
        for e in range(n):
            at = slice(e * CAP, (e + 1) * CAP)
            out[e, :, :width] = rows[at]
            out[e, :, width:] = jnp.zeros((CAP, BLK), BF16)
            out[e, :, width : width + ids.shape[1]] = listed[at]

    return call(
        body,
        jax.ShapeDtypeStruct((n, CAP, width + BLK), BF16),
        (tokens, route.reshape(1, count), blocks),
        "place_rows",
        False,
    )


def shift_rows(rows, dec):
    width = dec.shape[1]
    n = rows.shape[0]

    def body(x, d, out, kept):
        for e in range(n):
            at = slice(e * CAP, (e + 1) * CAP)
            kept[at, :] = x[e]
        out[:, :width] = (kept[:, :width].astype(F32) - d[...]).astype(BF16)
        out[:, width:] = kept[:, width:]

    shape = struct(n * CAP, rows.shape[2], BF16)
    return call(body, (shape, shape), (rows, dec), "shift_rows")


def join(outs, args, name):
    n = len(args)

    def body(*refs):
        for out, picks in zip(refs[n:], outs):
            at = 0
            for k in picks:
                rows = args[k].shape[0]
                out[at : at + rows, :] = refs[k][...]
                at += rows

    cols = args[0].shape[1]
    shapes = [struct(sum(args[k].shape[0] for k in picks), cols, BF16) for picks in outs]
    return call(body, shapes, args, name)


def gather_z(v):
    across, below, above = send(v, 0, 4), send(v, 0, 2), send(v, 0, -2)
    duo, a = join(((0, 1), (0, 1, 2, 3)), (v, across, below, above), "join_first")
    low, high = send(duo, 0, 1), send(duo, 0, -1)
    (b,) = join(((0, 1),), (low, high), "join_second")
    return a, b


def ring(a, b):
    r0, l1, r1, l0 = right(a), left(b), right(b), left(a)
    return (r0, r1, l0, l1), (right(r0), left(l1))


def big(body, outs, args, name, flops, in_specs=None):
    return pl.pallas_call(
        body,
        out_shape=outs,
        name=name,
        in_specs=in_specs or [ONCHIP] * len(args),
        out_specs=[ONCHIP] * len(outs),
        compiler_params=pltpu.CompilerParams(vmem_limit_bytes=12 << 20),
        cost_estimate=pl.CostEstimate(flops=flops, bytes_accessed=flops // 256, transcendentals=0),
    )(*args)


def forward(parts, weight, bias, index, out_types, name):
    n = len(parts)
    piece = parts[0].shape[0]
    rows = n * piece
    width, latents = weight.shape
    per = STEP // BLK

    def body(*refs):
        idx, ins, w, b = refs[0], refs[1 : 1 + n], refs[1 + n], refs[2 + n]
        s, a, m = refs[3 + n : 6 + n]
        outs = refs[6 + n :]
        for k in range(n):
            s[k * piece : (k + 1) * piece, :] = ins[k][:, :width]
        named = jnp.concatenate([r[:, width:] for r in ins], axis=0).astype(F32)
        for c in range(latents // STEP):
            at = slice(c * STEP, (c + 1) * STEP)
            pre = jnp.dot(s[...], w[:, at], preferred_element_type=F32) + b[:, at]
            base = (idx[0] * (latents // BLK) + c * per + 1).astype(F32)
            hits = []
            for j in range(per):
                found = jnp.max(jnp.where(named == base + j, 1.0, 0.0), axis=1, keepdims=True)
                hits.append(jnp.broadcast_to(found, (rows, BLK)))
            gate = jnp.where(pre > 0.0, jnp.concatenate(hits, axis=1), 0.0)
            a[:, at] = (jnp.maximum(pre, 0.0) * gate).astype(BF16)
            m[:, at] = gate.astype(BF16)
        for d in range(width // WIDE):
            at = slice(d * WIDE, (d + 1) * WIDE)
            part = lax.dot_general(a[...], w[at, :], PAIR, preferred_element_type=F32)
            for k in range(n):
                outs[k][:, at] = part[k * piece : (k + 1) * piece].astype(outs[k].dtype)

    specs = [pl.BlockSpec(memory_space=pltpu.SMEM)]
    specs += [ONCHIP] * (n + 2)
    outs = [
        struct(rows, width, BF16),
        struct(rows, latents, BF16),
        struct(rows, latents, BF16),
    ] + [struct(piece, width, t) for t in out_types]
    flops = 4 * rows * width * latents
    return big(body, outs, (index, *parts, weight, bias), name, flops, specs)


def backward(parts, weight, gate, bias, terms, name, after=()):
    n = len(parts)
    piece = parts[0].shape[0]
    rows = n * piece
    width, latents = weight.shape
    last = terms is not None

    def body(*refs):
        ins, w, m, prior = refs[:n], refs[n], refs[n + 1], refs[n + 2]
        rest = refs[n + 3 + len(after) :]
        if last:
            t, e, g, total, vec = rest
        else:
            e, g, total = rest
        for k in range(n):
            e[k * piece : (k + 1) * piece, :] = ins[k][...]
        for c in range(latents // STEP):
            at = slice(c * STEP, (c + 1) * STEP)
            grad = jnp.dot(e[...], w[:, at], preferred_element_type=F32) * m[:, at].astype(F32)
            g[:, at] = grad.astype(BF16)
            total[:, at] = jnp.sum(grad, axis=0, keepdims=True) + prior[:, at]
        if last:
            column = total[...].astype(BF16).astype(F32)
            column = jnp.broadcast_to(column, (8, latents)).astype(BF16)
            for d in range(width // WIDE):
                at = slice(d * WIDE, (d + 1) * WIDE)
                pulled = lax.dot_general(column, w[at, :], PAIR, preferred_element_type=F32)
                vec[:, at] = t[:, at] - pulled[:1]
            vec[:, width:] = t[:, width:]

    outs = [struct(rows, width, BF16), struct(rows, latents, BF16), struct(1, latents, F32)]
    args = (*parts, weight, gate, bias, *after)
    if last:
        outs += [struct(*terms.shape, F32)]
        args += (terms,)
    return big(body, outs, args, name, 2 * rows * width * latents)


def split_sum(own, a1, b1, a2, b2):
    half, width = a1.shape
    n = half // 4

    def body(pa, pb, w, x, y, z, mine, across, below, above, low, high):
        def rows(p, u, v, lo, count):
            at = slice(lo * n, (lo + count) * n)
            return p[at, :] + u[at, :].astype(F32) + v[at, :].astype(F32)

        low[...] = rows(pb, y, z, 0, 2).astype(BF16)
        high[...] = rows(pb, y, z, 2, 2).astype(BF16)
        below[...] = rows(pa, w, x, 2, 1).astype(BF16)
        above[...] = rows(pa, w, x, 3, 1).astype(BF16)
        mine[...] = rows(pa, w, x, 0, 1)
        across[...] = rows(pa, w, x, 1, 1)

    outs = [struct(n, width, F32)] * 2 + [struct(n, width, BF16)] * 2
    outs += [struct(2 * n, width, BF16)] * 2
    return call(body, outs, (*own, a1, b1, a2, b2), "split_sum")


def fold(across, low, high):
    n, width = across.shape

    def body(p, u, v, out):
        out[...] = (p[...] + u[n:, :].astype(F32) + v[n:, :].astype(F32)).astype(BF16)

    return call(body, struct(n, width, BF16), (across, low, high), "fold")


def form_error(own, others, rows, dec):
    share, width = own.shape

    def body(o, *refs):
        x, d, err, terms = refs[-4:]
        recon = o[...]
        for r in refs[:-4]:
            recon = recon + r[:share, :].astype(F32)
        held = jnp.where(x[:, width : width + 1].astype(F32) > 0.0, 1.0, 0.0)
        e = (recon + d[...] - x[:, :width].astype(F32)) * held
        err[...] = e.astype(BF16)
        terms[:, :width] = jnp.sum(e, axis=0, keepdims=True)
        loss = 0.5 * jnp.sum(jnp.sum(e * e, axis=1, keepdims=True), axis=0, keepdims=True)
        terms[:, width:] = jnp.broadcast_to(loss, (1, BLK))

    return call(
        body,
        (struct(share, width, BF16), struct(1, width + BLK, F32)),
        (own, *others, rows, dec),
        "form_error",
    )


def add_grad(acc, pairs, name):
    width, latents = pairs[0][0].shape[1], pairs[0][1].shape[1]
    flat = [v for pair in pairs for v in pair]
    kept = [] if acc is None else [acc]

    def body(*refs):
        out, mark = refs[-2:]
        mark[...] = jnp.zeros_like(mark)
        for d in range(width // STEP):
            at = slice(d * STEP, (d + 1) * STEP)
            total = refs[len(flat)][at, :] if kept else None
            for k in range(0, len(flat), 2):
                part = lax.dot_general(
                    refs[k][:, at], refs[k + 1][...], ROWS, preferred_element_type=F32
                )
                total = part if total is None else total + part
            out[at, :] = total

    rows = sum(u.shape[0] for u, _ in pairs)
    return pl.pallas_call(
        body,
        out_shape=[struct(width, latents, F32), struct(8, BLK, F32)],
        name=name,
        in_specs=[ONCHIP] * (len(flat) + len(kept)),
        out_specs=[ONCHIP] * 2,
        input_output_aliases={len(flat): 0} if kept else {},
        compiler_params=pltpu.CompilerParams(vmem_limit_bytes=12 << 20),
        cost_estimate=pl.CostEstimate(
            flops=2 * rows * width * latents, bytes_accessed=8 * width * latents, transcendentals=0
        ),
    )(*flat, *kept)


def finish_grad(buffer, first, count, acc, pairs):
    width, latents = acc.shape
    flat = [v for pair in pairs for v in pair]
    n = len(flat)
    kept = [] if buffer is None else [buffer]

    def body(*refs):
        at = pl.ds((first + pl.program_id(0)) * STEP, STEP)
        left_side = jnp.concatenate([refs[k][:, at] for k in range(0, n, 2)], axis=0)
        right_side = jnp.concatenate([refs[k][...] for k in range(1, n, 2)], axis=0)
        part = lax.dot_general(left_side, right_side, ROWS, preferred_element_type=F32)
        refs[-1][...] = (refs[n][at, :] + part).astype(BF16)

    rows = sum(u.shape[0] for u, _ in pairs)
    return pl.pallas_call(
        body,
        name="finish_grad",
        grid=(count,),
        in_specs=[ONCHIP] * (n + 1) + [pl.BlockSpec(memory_space=pl.ANY)] * len(kept),
        out_specs=pl.BlockSpec((STEP, latents), lambda c: (first + c, 0)),
        out_shape=struct(width, latents, BF16),
        input_output_aliases={n + 1: 0} if kept else {},
        compiler_params=pltpu.CompilerParams(vmem_limit_bytes=8 << 20),
        cost_estimate=pl.CostEstimate(
            flops=2 * rows * count * STEP * latents,
            bytes_accessed=6 * count * STEP * latents,
            transcendentals=0,
        ),
    )(*flat, acc, *kept)


def shards(tokens, route, blocks, weight, enc_bias, dec_bias):
    n_expert = lax.axis_size("expert")
    n_latent = lax.axis_size("latent")
    count, width = tokens.shape
    w = weight[0]
    latents = w.shape[1]
    share = n_expert * CAP
    dec = dec_bias[None]
    index = lax.axis_index("latent").astype(jnp.int32)[None]

    rows = place_rows(tokens, route, blocks)
    rows = lax.all_to_all(rows, "expert", split_axis=0, concat_axis=0, tiled=True)
    parcel, rows = shift_rows(rows, dec)
    za, zb = gather_z(parcel)
    near, far = ring(za, zb)
    s0, a0, m0, p0a, p0b = forward((za, zb), w, enc_bias, index, (F32, F32), "forward_own")
    index, _ = lax.optimization_barrier((index, p0a))
    s1, a1, m1, m_h1, m_h2, p_h1, p_h2 = forward(
        near, w, enc_bias, index, (BF16, F32, F32, BF16), "forward_near"
    )
    index, _ = lax.optimization_barrier((index, p_h1))
    s2, a2, m2, o_h1, o_h2 = forward(far, w, enc_bias, index, (BF16, BF16), "forward_far")
    in_a2, in_b1 = right(p_h2), left(m_h1)
    x1, x2 = right(o_h1), left(o_h2)
    in_a1 = right((p_h1 + x1.astype(F32)).astype(BF16))
    in_b2 = left((m_h2 + x2.astype(F32)).astype(BF16))
    mine, across, below, above, low, high = split_sum((p0a, p0b), in_a1, in_b1, in_a2, in_b2)
    low, high = send(low, 0, -1), send(high, 0, 1)
    others = (low, high, send(below, 0, -2), send(above, 0, 2))
    others += (send(fold(across, low, high), 0, 4),)
    error, terms = form_error(mine, others, rows, dec)

    ea, eb = gather_z(error)
    e_near, e_far = ring(ea, eb)
    zero = jnp.zeros((1, latents), F32)
    e0, g0, bias = backward((ea, eb), w, m0, zero, None, "backward_own")
    acc, mark = add_grad(None, ((s0, g0), (e0, a0)), "add_grad_own")
    e1, g1, bias = backward(e_near, w, m1, bias, None, "backward_near", (mark,))
    acc, mark = add_grad(acc, ((s1, g1), (e1, a1)), "add_grad_near")
    e2, g2, bias, vec = backward(e_far, w, m2, bias, terms, "backward_far", (mark,))

    tiles = width // STEP
    grad = None
    both = ("expert", "latent")
    stages = ((64, 128), (8, 16), (1, 2), (32,), (4,))
    for k, bits in enumerate(stages):
        masks = bits + ((bits[0] | bits[1],) if len(bits) == 2 else ())
        moved = [
            lax.ppermute(vec, both, [(i, i ^ m) for i in range(n_expert * n_latent)])
            for m in masks
        ]
        start, stop = tiles * k // len(stages), tiles * (k + 1) // len(stages)
        grad = finish_grad(grad, start, stop - start, acc, ((s2, g2), (e2, a2)))
        vec = vec + moved[0]
        if len(bits) == 2:
            vec = vec + (moved[1] + moved[2])
        vec, grad = lax.optimization_barrier((vec, grad))
    loss = vec[0, width] / (count * n_expert * n_latent)
    return (grad[None], bias, vec[0, :width], loss)


def solution(mesh):
    return jax.shard_map(
        shards,
        mesh=mesh,
        in_specs=(
            P(("expert", "latent"), None),
            P(("expert", "latent"), None),
            P(("expert", "latent"), None),
            P("expert", None, "latent"),
            P("expert", "latent"),
            P(),
        ),
        out_specs=(P("expert", None, "latent"), P("expert", "latent"), P(), P()),
        check_vma=False,
    )
```
